32 devices in a mesh: dp: 16 (over z, y, x), tensor: 2 (over core).
Axes of the slice: x: 2, y: 2, z: 4, core: 2. Of those that a mesh axis runs over, the one named last changes fastest.
Arguments:
- tokens: bfloat16 [4096, 1024], P(('dp', 'tensor')), may hold values from -6 to 6
- cotangent: bfloat16 [4096, 1024], P(('dp', 'tensor')), may hold values from -6 to 6
- seq_lengths: int32 [16, 4], P('dp'), may hold values from 1 to 128, as said below
- seq_offsets: int32 [16, 4], P('dp'), may hold values from 0 to 192, as said below
- token_counts: int32 [16], replicated, may hold values from 1 to 224, as said below
- qkv_weight: float32 [3, 1024, 1024], P(None, 'dp', 'tensor'), may hold values from -1 to 1
- out_weight: float32 [1024, 1024], P('dp', 'tensor'), may hold values from -0.75 to 0.75
- fc1_weight: float32 [1024, 4096], P('dp', 'tensor'), may hold values from -0.1875 to 0.1875
- fc2_weight: float32 [1024, 4096], P('dp', 'tensor'), may hold values from -0.09375 to 0.09375
- vectors: float32 [12, 1024], P(None, 'dp'), may hold values from -1 to 1.3
- qkv_first: float32 [3, 1024, 1024], P(None, 'dp', 'tensor'), may hold values from -0.0234375 to 0.0234375
- qkv_second: float32 [3, 1024, 1024], P(None, 'dp', 'tensor'), may hold values from 4.882813e-07 to 9.765625e-06
- out_first: float32 [1024, 1024], P('dp', 'tensor'), may hold values from -0.0234375 to 0.0234375
- out_second: float32 [1024, 1024], P('dp', 'tensor'), may hold values from 4.882813e-07 to 9.765625e-06
- fc1_first: float32 [1024, 4096], P('dp', 'tensor'), may hold values from -0.0234375 to 0.0234375
- fc1_second: float32 [1024, 4096], P('dp', 'tensor'), may hold values from 4.882813e-07 to 9.765625e-06
- fc2_first: float32 [1024, 4096], P('dp', 'tensor'), may hold values from -0.0234375 to 0.0234375
- fc2_second: float32 [1024, 4096], P('dp', 'tensor'), may hold values from 4.882813e-07 to 9.765625e-06
- vector_first: float32 [12, 1024], P(None, 'dp'), may hold values from -0.0234375 to 0.0234375
- vector_second: float32 [12, 1024], P(None, 'dp'), may hold values from 4.882813e-07 to 9.765625e-06
Outputs:
- output: float32 [4096, 1024], P(('dp', 'tensor'))
- input_grad: float32 [4096, 1024], P(('dp', 'tensor'))
- qkv_grad: float32 [3, 1024, 1024], P(None, 'dp', 'tensor')
- out_grad: float32 [1024, 1024], P('dp', 'tensor')
- fc1_grad: float32 [1024, 4096], P('dp', 'tensor')
- fc2_grad: float32 [1024, 4096], P('dp', 'tensor')
- vector_grad: float32 [12, 1024], P(None, 'dp')
- qkv_new: float32 [3, 1024, 1024], P(None, 'dp', 'tensor')
- out_new: float32 [1024, 1024], P('dp', 'tensor')
- fc1_new: float32 [1024, 4096], P('dp', 'tensor')
- fc2_new: float32 [1024, 4096], P('dp', 'tensor')
- vector_new: float32 [12, 1024], P(None, 'dp')
- qkv_first_new: float32 [3, 1024, 1024], P(None, 'dp', 'tensor')
- qkv_second_new: float32 [3, 1024, 1024], P(None, 'dp', 'tensor')
- out_first_new: float32 [1024, 1024], P('dp', 'tensor')
- out_second_new: float32 [1024, 1024], P('dp', 'tensor')
- fc1_first_new: float32 [1024, 4096], P('dp', 'tensor')
- fc1_second_new: float32 [1024, 4096], P('dp', 'tensor')
- fc2_first_new: float32 [1024, 4096], P('dp', 'tensor')
- fc2_second_new: float32 [1024, 4096], P('dp', 'tensor')
- vector_first_new: float32 [12, 1024], P(None, 'dp')
- vector_second_new: float32 [12, 1024], P(None, 'dp')
The draws below stay inside these ranges and needn't reach their ends.
Inputs may be any that keep to these rules, and one draw needn't show every extreme that they name: Sequence s of group g occupies local rows seq_offsets[g, s] to seq_offsets[g, s] + seq_lengths[g, s] - 1, all below 256; some group has a sequence of 128 tokens. `seq_offsets`: the first offset of a group is 0; each later one is the previous sequence's end rounded up to a multiple of 16. token_counts[g] is the end of group g's last sequence.
All inputs are finite; a program needn't handle non-finite values.
Results may differ from the reference program's by a relative error of at most 0.025.
The reference program's roundings to bfloat16 on the way count: a program that leaves them out, or rounds other values in their place, can miss the bound.
Values may be sent and summed in bfloat16 or wider, within the bound.
A program may use at most 128 MiB of HBM per device.

```python
import math
import jax
import jax.numpy as jnp
from jax import lax

D = 1024
HEADS = 16
FF = 4096
HEAD_DIM = 64
CAP = 256
SEQS = 4
PAD = 16
STEP = 3
MAXLEN = 128
SHORT = 32
VROWS = 12
GROUPS = 16
TOKENS = 4096


def layout_tables(key):
    base = jax.random.fold_in(key, 11)
    first_key, rest_key, pick_key = jax.random.split(base, 3)
    first_len = jax.random.randint(first_key, (GROUPS, 1), PAD, MAXLEN + 1)
    rest_len = jax.random.randint(rest_key, (GROUPS, SEQS - 1), 1, SHORT + 1)
    chosen = jax.random.randint(pick_key, (), 0, GROUPS)
    is_chosen = jnp.arange(GROUPS)[:, None] == chosen
    first_len = jnp.where(is_chosen, MAXLEN, first_len)
    rest_len = jnp.where(is_chosen, SHORT, rest_len)
    lengths = jnp.concatenate([first_len, rest_len], axis=1).astype(jnp.int32)
    padded = ((lengths + PAD - 1) // PAD * PAD).astype(jnp.int32)
    offsets = (jnp.cumsum(padded, axis=1) - padded).astype(jnp.int32)
    counts = (offsets[:, -1] + lengths[:, -1]).astype(jnp.int32)
    return (lengths, offsets, counts)


def draw_seq_lengths(key, part):
    return layout_tables(key)[0]


def draw_seq_offsets(key, part):
    return layout_tables(key)[1]


def draw_token_counts(key, part):
    return layout_tables(key)[2]


def draw_qkv_weight(key, part):
    base_key = jax.random.fold_in(jax.random.fold_in(key, 23), 0)
    spread = D ** (-0.5)
    return jax.random.truncated_normal(base_key, -4.0, 4.0, (3, D, D), jnp.float32) * spread


def draw_vectors(key, part):
    gain_key, shift_key = jax.random.split(jax.random.fold_in(key, 37))
    gains = jax.random.uniform(gain_key, (VROWS, D), jnp.float32, 0.7, 1.3)
    shifts = 0.3 * jax.random.truncated_normal(shift_key, -3.0, 3.0, (VROWS, D), jnp.float32)
    row_ids = jnp.arange(VROWS)[:, None]
    return jnp.where((row_ids == 0) | (row_ids == 5), gains, shifts)


def block_levels(rng, extent, cuts, smallest, largest):
    def one(dim, shards_of):
        heights = jax.random.uniform(jax.random.fold_in(jax.random.fold_in(rng, 6), dim), (shards_of,), jnp.float32, smallest / len(cuts), largest / len(cuts))
        return jnp.repeat(jnp.exp(heights), extent[dim] // shards_of).reshape((-1,) + (1,) * (len(extent) - dim - 1))

    level = one(*cuts[0])
    for cut in cuts[1:]:
        level = level * one(*cut)
    return level


def gaussian(own_key, extent, width, bound, cuts=(), kind=jnp.bfloat16):
    values = width * jax.random.normal(own_key, extent, jnp.float32)
    if cuts:
        values = values * block_levels(own_key, extent, cuts, -0.22, 0.18)
    return jnp.clip(values, -bound, bound).astype(kind)


def setup_inputs(seed: int = 0) -> dict:
    seeds = jax.random.split(jax.random.key(seed), 21)
    tokens = gaussian(seeds[0], (TOKENS, D), 1.0, 6.0, ((0, 32),))
    cotangent = gaussian(seeds[1], (TOKENS, D), 1.0, 6.0, ((0, 32),))
    seq_lengths = draw_seq_lengths(jax.random.fold_in(seeds[20], 71), 0)
    seq_offsets = draw_seq_offsets(jax.random.fold_in(seeds[20], 71), 0)
    token_counts = draw_token_counts(jax.random.fold_in(seeds[20], 71), 0)
    qkv_weight = draw_qkv_weight(jax.random.fold_in(seeds[20], 71), 0)
    out_weight = gaussian(seeds[6], (D, D), (D // 16) ** -0.5, 0.75, ((0, 16), (1, 2)), jnp.float32)
    fc1_weight = gaussian(seeds[7], (D, FF), D ** -0.5, 0.1875, ((0, 16), (1, 2)), jnp.float32)
    fc2_weight = gaussian(seeds[8], (D, FF), FF ** -0.5, 0.09375, ((0, 16), (1, 2)), jnp.float32)
    vectors = draw_vectors(jax.random.fold_in(seeds[20], 71), 0)
    qkv_first = gaussian(seeds[10], (3, D, D), (0.3 * TOKENS ** -0.5), 0.0234375, ((1, 16), (2, 2)), jnp.float32)
    qkv_second = jnp.clip(jnp.exp(math.log(9.765624781721272e-06) - 2.9957322 * jax.random.uniform(seeds[11], (3, D, D), jnp.float32) ** block_levels(seeds[11], (3, D, D), ((1, 16), (2, 2)), -0.2, 0.2)), 4.882812731921149e-07, 9.765624781721272e-06)
    out_first = gaussian(seeds[12], (D, D), (0.3 * TOKENS ** -0.5), 0.0234375, ((0, 16), (1, 2)), jnp.float32)
    out_second = jnp.clip(jnp.exp(math.log(9.765624781721272e-06) - 2.9957322 * jax.random.uniform(seeds[13], (D, D), jnp.float32) ** block_levels(seeds[13], (D, D), ((0, 16), (1, 2)), -0.2, 0.2)), 4.882812731921149e-07, 9.765624781721272e-06)
    fc1_first = gaussian(seeds[14], (D, FF), (0.3 * TOKENS ** -0.5), 0.0234375, ((0, 16), (1, 2)), jnp.float32)
    fc1_second = jnp.clip(jnp.exp(math.log(9.765624781721272e-06) - 2.9957322 * jax.random.uniform(seeds[15], (D, FF), jnp.float32) ** block_levels(seeds[15], (D, FF), ((0, 16), (1, 2)), -0.2, 0.2)), 4.882812731921149e-07, 9.765624781721272e-06)
    fc2_first = gaussian(seeds[16], (D, FF), (0.3 * TOKENS ** -0.5), 0.0234375, ((0, 16), (1, 2)), jnp.float32)
    fc2_second = jnp.clip(jnp.exp(math.log(9.765624781721272e-06) - 2.9957322 * jax.random.uniform(seeds[17], (D, FF), jnp.float32) ** block_levels(seeds[17], (D, FF), ((0, 16), (1, 2)), -0.2, 0.2)), 4.882812731921149e-07, 9.765624781721272e-06)
    vector_first = gaussian(seeds[18], (VROWS, D), (0.3 * TOKENS ** -0.5), 0.0234375, ((1, 16),), jnp.float32)
    vector_second = jnp.clip(jnp.exp(math.log(9.765624781721272e-06) - 2.9957322 * jax.random.uniform(seeds[19], (VROWS, D), jnp.float32) ** block_levels(seeds[19], (VROWS, D), ((1, 16),), -0.2, 0.2)), 4.882812731921149e-07, 9.765624781721272e-06)
    return {"tokens": tokens, "cotangent": cotangent, "seq_lengths": seq_lengths, "seq_offsets": seq_offsets, "token_counts": token_counts, "qkv_weight": qkv_weight, "out_weight": out_weight, "fc1_weight": fc1_weight, "fc2_weight": fc2_weight, "vectors": vectors, "qkv_first": qkv_first, "qkv_second": qkv_second, "out_first": out_first, "out_second": out_second, "fc1_first": fc1_first, "fc1_second": fc1_second, "fc2_first": fc2_first, "fc2_second": fc2_second, "vector_first": vector_first, "vector_second": vector_second}


HALF_TYPE = jnp.bfloat16
FULL_TYPE = jnp.float32
GELU_SCALE = 0.7978845608028654
GELU_CUBIC = 0.044715
NORM_EPS = 1e-05
BETA_ONE = 0.9
BETA_TWO = 0.95
LEARN_RATE = 0.05
DECAY_RATE = 0.1
ADAM_EPS = 1e-08
NEG_LARGE = -1e+30

def rounded(matrix):
    return lax.optimization_barrier(matrix.astype(HALF_TYPE))

def norm_rows(matrix):
    center = matrix - lax.optimization_barrier(jnp.mean(matrix, axis=-1, keepdims=True))
    inv_root = lax.rsqrt(lax.optimization_barrier(jnp.mean(center * center, axis=-1, keepdims=True)) + NORM_EPS)
    return (center * inv_root, inv_root)

def norm_back(gradient, normed, inv_root, gain):
    inner_grad = gradient * gain
    return inv_root * (inner_grad - lax.optimization_barrier(jnp.mean(inner_grad, axis=-1, keepdims=True)) - normed * lax.optimization_barrier(jnp.mean(inner_grad * normed, axis=-1, keepdims=True)))

def gelu_value(pre_act):
    return 0.5 * pre_act * (1.0 + jnp.tanh(GELU_SCALE * (pre_act + GELU_CUBIC * pre_act * pre_act * pre_act)))

def gelu_slope(pre_act):
    tangent = jnp.tanh(GELU_SCALE * (pre_act + GELU_CUBIC * pre_act * pre_act * pre_act))
    return 0.5 * (1.0 + tangent) + 0.5 * pre_act * (1.0 - tangent * tangent) * GELU_SCALE * (1.0 + 3.0 * GELU_CUBIC * pre_act * pre_act)

def row_labels(lengths, offsets, group_rows):
    places = jnp.arange(group_rows, dtype=jnp.int32)[:, None]
    inside = (places >= offsets[None, :]) & (places < offsets[None, :] + lengths[None, :])
    rank_ids = jnp.arange(lengths.shape[0], dtype=jnp.int32)[None, :] + 1
    return (lax.optimization_barrier(jnp.sum(jnp.where(inside, rank_ids, 0), axis=1)) - 1).astype(jnp.int32)

def score_table(queries, key_rows, slopes, labels):
    raw_scores = jnp.einsum('qhd,khd->hqk', queries, key_rows) * queries.shape[2] ** (-0.5)
    places = jnp.arange(queries.shape[0], dtype=jnp.int32)
    row_gap = places[:, None] - places[None, :]
    allowed = (labels[:, None] == labels[None, :]) & (row_gap >= 0)
    return jnp.where(allowed[None], raw_scores - slopes[:, None, None] * row_gap.astype(FULL_TYPE)[None], NEG_LARGE)

def adam_step(weight, first_moment, second_moment, gradient, decay_rate):
    first_new = BETA_ONE * first_moment + (1.0 - BETA_ONE) * gradient
    second_new = BETA_TWO * second_moment + (1.0 - BETA_TWO) * gradient * gradient
    first_hat = first_new / (1.0 - BETA_ONE ** STEP)
    second_hat = second_new / (1.0 - BETA_TWO ** STEP)
    weight_new = weight - LEARN_RATE * (first_hat / (jnp.sqrt(second_hat) + ADAM_EPS) + decay_rate * weight)
    return (weight_new, first_new, second_new)

def reference(tokens, cotangent, seq_lengths, seq_offsets, token_counts, qkv_weight, out_weight, fc1_weight, fc2_weight, vectors, qkv_first, qkv_second, out_first, out_second, fc1_first, fc1_second, fc2_first, fc2_second, vector_first, vector_second):
    w_qkv = rounded(qkv_weight).astype(FULL_TYPE)
    w_out = rounded(out_weight)
    w_up = rounded(fc1_weight)
    w_down = rounded(fc2_weight)
    vector_rows = rounded(vectors).astype(FULL_TYPE)
    up_rows = FF // D
    down_row = 7 + up_rows
    up_bias = vector_rows[7:down_row].reshape(FF)
    slopes = jnp.exp2(-8.0 * (jnp.arange(HEADS) + 1).astype(FULL_TYPE) / HEADS)
    inv_scale = HEAD_DIM ** (-0.5)

    def one_group(carry, group):
        x_rows, grad_in, lengths, offsets, count_now = group
        labels = row_labels(lengths, offsets, CAP)
        valid = (labels >= 0) & (jnp.arange(CAP, dtype=jnp.int32) < count_now)
        x_full = x_rows.astype(FULL_TYPE)
        normed1, inv1 = norm_rows(x_full)
        h_one = rounded(normed1 * vector_rows[0] + vector_rows[1]).astype(FULL_TYPE)
        projected = jnp.einsum('rd,cde->cre', h_one, w_qkv)
        queries = rounded(projected[0] + vector_rows[2]).astype(FULL_TYPE).reshape(CAP, HEADS, HEAD_DIM)
        key_rows = rounded(projected[1]).astype(FULL_TYPE).reshape(CAP, HEADS, HEAD_DIM)
        values = rounded(projected[2] + vector_rows[3]).astype(FULL_TYPE).reshape(CAP, HEADS, HEAD_DIM)
        scores = score_table(queries, key_rows, slopes, labels)
        row_peak = lax.optimization_barrier(jnp.max(scores, axis=2, keepdims=True))
        log_total = row_peak + jnp.log(lax.optimization_barrier(jnp.sum(jnp.exp(scores - row_peak), axis=2, keepdims=True)))
        prob_table = jnp.exp(scores - log_total)
        prob_half = rounded(prob_table).astype(FULL_TYPE)
        mixed_heads = rounded(jnp.einsum('hqk,khd->qhd', prob_half, values)).reshape(CAP, D)
        residual = x_full + jnp.dot(mixed_heads, w_out.T, preferred_element_type=FULL_TYPE) + vector_rows[4]
        normed2, inv2 = norm_rows(residual)
        h_two = rounded(normed2 * vector_rows[5] + vector_rows[6])
        pre_act = jnp.dot(h_two, w_up, preferred_element_type=FULL_TYPE) + up_bias
        activation = rounded(gelu_value(pre_act))
        output = jnp.where(valid[:, None], residual + jnp.dot(activation, w_down.T, preferred_element_type=FULL_TYPE) + vector_rows[down_row], 0.0)
        grad_out = jnp.where(valid[:, None], grad_in.astype(FULL_TYPE), 0.0)
        grad_half = rounded(grad_out)
        grad_pre = jnp.dot(grad_half, w_down, preferred_element_type=FULL_TYPE) * gelu_slope(pre_act)
        grad_pre_half = rounded(grad_pre)
        grad_down = jnp.dot(grad_half.T, activation, preferred_element_type=FULL_TYPE)
        grad_up = jnp.dot(h_two.T, grad_pre_half, preferred_element_type=FULL_TYPE)
        grad_h2 = jnp.dot(grad_pre_half, w_up.T, preferred_element_type=FULL_TYPE)
        grad_resid = grad_out + norm_back(grad_h2, normed2, inv2, vector_rows[5])
        resid_half = rounded(grad_resid)
        grad_outw = jnp.dot(resid_half.T, mixed_heads, preferred_element_type=FULL_TYPE)
        grad_mixed = rounded(jnp.dot(resid_half, w_out, preferred_element_type=FULL_TYPE)).astype(FULL_TYPE).reshape(CAP, HEADS, HEAD_DIM)
        mixed_full = mixed_heads.astype(FULL_TYPE).reshape(CAP, HEADS, HEAD_DIM)
        delta_rows = jnp.einsum('qhd,qhd->hq', grad_mixed, mixed_full)
        grad_probs = jnp.einsum('qhd,khd->hqk', grad_mixed, values)
        grad_scores = rounded(prob_table * (grad_probs - delta_rows[:, :, None])).astype(FULL_TYPE)
        grad_q = jnp.einsum('hqk,khd->qhd', grad_scores, key_rows) * inv_scale
        grad_k = jnp.einsum('hqk,qhd->khd', grad_scores, queries) * inv_scale
        grad_v = jnp.einsum('hqk,qhd->khd', prob_half, grad_mixed)
        grad_proj = jnp.stack([grad_q, grad_k, grad_v]).reshape(3, CAP, D)
        grad_proj_half = rounded(grad_proj).astype(FULL_TYPE)
        grad_qkv = jnp.einsum('rd,cre->cde', h_one, grad_proj_half)
        grad_h1 = jnp.einsum('cre,cde->rd', grad_proj_half, w_qkv)
        grad_tokens = grad_resid + norm_back(grad_h1, normed1, inv1, vector_rows[0])
        head_part = jnp.stack([lax.optimization_barrier(jnp.sum(grad_h1 * normed1, axis=0)), lax.optimization_barrier(jnp.sum(grad_h1, axis=0)), lax.optimization_barrier(jnp.sum(grad_proj[0], axis=0)), lax.optimization_barrier(jnp.sum(grad_proj[2], axis=0)), lax.optimization_barrier(jnp.sum(grad_resid, axis=0)), lax.optimization_barrier(jnp.sum(grad_h2 * normed2, axis=0)), lax.optimization_barrier(jnp.sum(grad_h2, axis=0))])
        grad_vec = jnp.concatenate([head_part, lax.optimization_barrier(jnp.sum(grad_pre, axis=0)).reshape(up_rows, D), lax.optimization_barrier(jnp.sum(grad_out, axis=0))[None]], axis=0)
        terms = (grad_qkv, grad_outw, grad_up, grad_down, grad_vec)
        carry = tuple((held + term for held, term in zip(carry, terms)))
        return (carry, (output, grad_tokens))
    start = (jnp.zeros((3, D, D), FULL_TYPE), jnp.zeros((D, D), FULL_TYPE), jnp.zeros((D, FF), FULL_TYPE), jnp.zeros((D, FF), FULL_TYPE), jnp.zeros((VROWS, D), FULL_TYPE))
    groups = (tokens.reshape(GROUPS, CAP, D), cotangent.reshape(GROUPS, CAP, D), seq_lengths, seq_offsets, token_counts)
    sums, (outputs, grads_in) = lax.scan(one_group, start, groups)
    token_total = jnp.sum(token_counts).astype(FULL_TYPE)
    qkv_grad, out_grad, fc1_grad, fc2_grad, vector_grad = [held / token_total for held in sums]
    qkv_new, qkv_first_new, qkv_second_new = adam_step(qkv_weight, qkv_first, qkv_second, qkv_grad, DECAY_RATE)
    out_new, out_first_new, out_second_new = adam_step(out_weight, out_first, out_second, out_grad, DECAY_RATE)
    fc1_new, fc1_first_new, fc1_second_new = adam_step(fc1_weight, fc1_first, fc1_second, fc1_grad, DECAY_RATE)
    fc2_new, fc2_first_new, fc2_second_new = adam_step(fc2_weight, fc2_first, fc2_second, fc2_grad, DECAY_RATE)
    vector_new, vector_first_new, vector_second_new = adam_step(vectors, vector_first, vector_second, vector_grad, 0.0)
    return (outputs.reshape(TOKENS, D), grads_in.reshape(TOKENS, D), qkv_grad, out_grad, fc1_grad, fc2_grad, vector_grad, qkv_new, out_new, fc1_new, fc2_new, vector_new, qkv_first_new, qkv_second_new, out_first_new, out_second_new, fc1_first_new, fc1_second_new, fc2_first_new, fc2_second_new, vector_first_new, vector_second_new)
```

```python
import jax
import jax.numpy as jnp
from jax import lax
from jax.sharding import PartitionSpec as P

HEADS = 16
HEAD_DIM = 64
STEP = 3


HALF_TYPE = jnp.bfloat16
FULL_TYPE = jnp.float32
GELU_SCALE = 0.7978845608028654
GELU_CUBIC = 0.044715
NORM_EPS = 1e-05
BETA_ONE = 0.9
BETA_TWO = 0.95
LEARN_RATE = 0.05
DECAY_RATE = 0.1
ADAM_EPS = 1e-08
NEG_LARGE = -1e30


def axis_plan(size):
    factors, rest = [], size
    if rest % 4 == 0:
        factors.append(4)
        rest //= 4
    divisor = 2
    while rest > 1:
        while rest % divisor == 0:
            factors.append(divisor)
            rest //= divisor
        divisor += 1
    strides, stride = [], size
    for factor in factors:
        stride //= factor
        strides.append(stride)
    return factors, strides


def moves(size, factor, stride, step):
    pairs = []
    for source in range(size):
        coord = (source // stride) % factor
        pairs.append((source, source + ((coord + step) % factor - coord) * stride))
    return pairs


def gather_axis(block, place, factor, stride, size):
    coord = (lax.axis_index("dp") // stride) % factor
    held = [block] + [
        lax.ppermute(block, "dp", moves(size, factor, stride, step)) for step in range(1, factor)
    ]
    parts = []
    for slot in range(factor):
        part = held[0]
        for step in range(1, factor):
            part = jnp.where(coord == (slot + step) % factor, held[step], part)
        parts.append(part)
    return jnp.concatenate(parts, axis=place)


def scatter_axis(table, place, factor, stride, size):
    coord = (lax.axis_index("dp") // stride) % factor

    def take(step):
        return lax.dynamic_slice_in_dim(table, (coord + step) % factor, 1, axis=place)

    total = take(0).astype(FULL_TYPE)
    for step in range(1, factor):
        away = take(step).astype(HALF_TYPE)
        other = lax.ppermute(away, "dp", moves(size, factor, stride, step))
        total = total + other.astype(FULL_TYPE)
    return total


def stage_orders(count):
    forward = list(range(count))
    return [forward, forward[:1] + forward[1:][::-1]]


def gather_stage(block, place, size):
    factors, strides = axis_plan(size)
    return gather_axis(block, place, factors[place], strides[place], size)


def scatter_stage(table, place, size):
    factors, strides = axis_plan(size)
    return scatter_axis(table, place, factors[place], strides[place], size)


def tensor_scatter(rows, send_type):
    size = lax.axis_size("tensor")
    if size != 2:
        return lax.psum_scatter(rows, "tensor", scatter_dimension=0, tiled=True)
    half = rows.shape[0] // 2
    index = lax.axis_index("tensor")
    own = lax.dynamic_slice_in_dim(rows, index * half, half)
    away = lax.dynamic_slice_in_dim(rows, (1 - index) * half, half).astype(send_type)
    return own + lax.ppermute(away, "tensor", [(0, 1), (1, 0)]).astype(FULL_TYPE)


def norm_rows(matrix):
    center = matrix - jnp.mean(matrix, axis=-1, keepdims=True)
    inv_root = lax.rsqrt(jnp.mean(center * center, axis=-1, keepdims=True) + NORM_EPS)
    return (center * inv_root, inv_root)


def norm_back(gradient, normed, inv_root, gain):
    inner_grad = gradient * gain
    return inv_root * (
        inner_grad
        - jnp.mean(inner_grad, axis=-1, keepdims=True)
        - normed * jnp.mean(inner_grad * normed, axis=-1, keepdims=True)
    )


def gelu_value(pre_act):
    return (
        0.5
        * pre_act
        * (1.0 + jnp.tanh(GELU_SCALE * (pre_act + GELU_CUBIC * pre_act * pre_act * pre_act)))
    )


def gelu_slope(pre_act):
    tangent = jnp.tanh(GELU_SCALE * (pre_act + GELU_CUBIC * pre_act * pre_act * pre_act))
    return 0.5 * (1.0 + tangent) + 0.5 * pre_act * (1.0 - tangent * tangent) * GELU_SCALE * (
        1.0 + 3.0 * GELU_CUBIC * pre_act * pre_act
    )


def row_labels(lengths, offsets, group_rows):
    places = jnp.arange(group_rows, dtype=jnp.int32)[:, None]
    inside = (places >= offsets[None, :]) & (places < offsets[None, :] + lengths[None, :])
    rank_ids = jnp.arange(lengths.shape[0], dtype=jnp.int32)[None, :] + 1
    return jnp.sum(jnp.where(inside, rank_ids, 0), axis=1) - 1


def score_table(queries, key_rows, slopes, labels):
    raw_scores = jnp.einsum(
        "qhd,khd->hqk", queries, key_rows, preferred_element_type=FULL_TYPE
    ) * queries.shape[2] ** (-0.5)
    places = jnp.arange(queries.shape[0], dtype=jnp.int32)
    row_gap = places[:, None] - places[None, :]
    allowed = (labels[:, None] == labels[None, :]) & (row_gap >= 0)
    return jnp.where(
        allowed[None],
        raw_scores - slopes[:, None, None] * row_gap.astype(FULL_TYPE)[None],
        NEG_LARGE,
    )


def adam_step(weight, first_moment, second_moment, gradient, decay_rate):
    first_new = BETA_ONE * first_moment + (1.0 - BETA_ONE) * gradient
    second_new = BETA_TWO * second_moment + (1.0 - BETA_TWO) * gradient * gradient
    first_hat = first_new / (1.0 - BETA_ONE**STEP)
    second_hat = second_new / (1.0 - BETA_TWO**STEP)
    weight_new = weight - LEARN_RATE * (
        first_hat / (jnp.sqrt(second_hat) + ADAM_EPS) + decay_rate * weight
    )
    return (weight_new, first_new, second_new)


def local(
    tokens,
    cotangent,
    seq_lengths,
    seq_offsets,
    token_counts,
    qkv_weight,
    out_weight,
    fc1_weight,
    fc2_weight,
    vectors,
    qkv_first,
    qkv_second,
    out_first,
    out_second,
    fc1_first,
    fc1_second,
    fc2_first,
    fc2_second,
    vector_first,
    vector_second,
):
    tensor_size = lax.axis_size("tensor")
    tensor_index = lax.axis_index("tensor")
    share_rows = tokens.shape[0]
    group_rows = share_rows * tensor_size
    model_width = tokens.shape[1]
    head_cols = qkv_weight.shape[2]
    hidden_cols = fc1_weight.shape[1]
    local_heads = head_cols // HEAD_DIM
    up_rows = hidden_cols * tensor_size // model_width
    down_row = 7 + up_rows
    inv_scale = HEAD_DIM ** (-0.5)
    dp_size = lax.axis_size("dp")
    factors, _ = axis_plan(dp_size)
    stages = len(factors)
    ones = (1,) * stages
    orders = stage_orders(stages)
    shard = qkv_weight.shape[1]
    vec_rows, vec_cols = vectors.shape
    pad_rows = -vec_rows % 16
    vec_block = jnp.pad(
        vectors.astype(HALF_TYPE), ((0, pad_rows), (0, head_cols - vec_cols))
    )
    qkv_half = qkv_weight.astype(HALF_TYPE)
    near = [
        jnp.concatenate([qkv_half[0], qkv_half[1], vec_block], axis=0),
        jnp.concatenate([qkv_half[2], out_weight.astype(HALF_TYPE)], axis=0),
    ]
    far = [fc1_weight.astype(HALF_TYPE), fc2_weight.astype(HALF_TYPE)]
    near = [block.reshape(ones + block.shape) for block in near]
    far = [block.reshape(ones + block.shape) for block in far]
    near_rows = near[0].shape[-2]
    near = gather_stage(jnp.concatenate(near, axis=-2), 0, dp_size)
    near, far = lax.optimization_barrier((near, far))
    near = [near[..., :near_rows, :], near[..., near_rows:, :]]
    far = gather_stage(jnp.concatenate(far, axis=-2), 0, dp_size)
    for step in range(1, stages):
        near = [gather_stage(block, orders[i][step], dp_size) for i, block in enumerate(near)]
    far = [far[..., :shard, :], far[..., shard:, :]]
    for step in range(1, stages):
        far = [gather_stage(block, orders[i][step], dp_size) for i, block in enumerate(far)]
    full_rows = dp_size * shard
    first = near[0].reshape(dp_size, -1, head_cols)
    second = near[1].reshape(dp_size, -1, head_cols)
    w_qkv = [
        first[:, :shard].reshape(full_rows, head_cols),
        first[:, shard : 2 * shard].reshape(full_rows, head_cols),
        second[:, :shard].reshape(full_rows, head_cols),
    ]
    w_out = second[:, shard:].reshape(full_rows, head_cols)
    w_up = far[0].reshape(full_rows, hidden_cols)
    w_down = far[1].reshape(full_rows, hidden_cols)
    vector_half = (
        first[:, 2 * shard : 2 * shard + vec_rows, :vec_cols]
        .transpose(1, 0, 2)
        .reshape(vec_rows, dp_size * vec_cols)
    )
    vector_rows = vector_half.astype(FULL_TYPE)
    q_bias = lax.dynamic_slice_in_dim(vector_rows[2], tensor_index * head_cols, head_cols)
    v_bias = lax.dynamic_slice_in_dim(vector_rows[3], tensor_index * head_cols, head_cols)
    up_bias = lax.dynamic_slice_in_dim(
        vector_rows[7:down_row].reshape(-1), tensor_index * hidden_cols, hidden_cols
    )
    labels = row_labels(seq_lengths[0], seq_offsets[0], group_rows)
    share_start = tensor_index * share_rows
    share_labels = lax.dynamic_slice_in_dim(labels, share_start, share_rows)
    count_now = lax.dynamic_index_in_dim(token_counts, lax.axis_index("dp"), 0, keepdims=False)
    share_places = share_start + jnp.arange(share_rows, dtype=jnp.int32)
    valid = (share_labels >= 0) & (share_places < count_now)
    token_total = jnp.sum(token_counts).astype(FULL_TYPE)
    slopes = jnp.exp2(
        -8.0 * (tensor_index * local_heads + jnp.arange(local_heads) + 1).astype(FULL_TYPE) / HEADS
    )
    x_full = tokens.astype(FULL_TYPE)
    normed1, inv1 = norm_rows(x_full)
    h_one = lax.all_gather(
        (normed1 * vector_rows[0] + vector_rows[1]).astype(HALF_TYPE), "tensor", axis=0, tiled=True
    )
    projected = [jnp.dot(h_one, w, preferred_element_type=FULL_TYPE) for w in w_qkv]
    queries = (projected[0] + q_bias).astype(HALF_TYPE).reshape(group_rows, local_heads, HEAD_DIM)
    key_rows = projected[1].astype(HALF_TYPE).reshape(group_rows, local_heads, HEAD_DIM)
    values = (projected[2] + v_bias).astype(HALF_TYPE).reshape(group_rows, local_heads, HEAD_DIM)
    scores = score_table(queries, key_rows, slopes, labels)
    row_peak = jnp.max(scores, axis=2, keepdims=True)
    log_total = row_peak + jnp.log(jnp.sum(jnp.exp(scores - row_peak), axis=2, keepdims=True))
    prob_half = jnp.exp(scores - log_total).astype(HALF_TYPE)
    mixed_heads = (
        jnp.einsum("hqk,khd->qhd", prob_half, values, preferred_element_type=FULL_TYPE)
        .astype(HALF_TYPE)
        .reshape(group_rows, head_cols)
    )
    part_rows = mixed_heads
    attn_share = tensor_scatter(
        lax.dot_general(
            part_rows, w_out, (((1,), (1,)), ((), ())), preferred_element_type=FULL_TYPE
        ),
        FULL_TYPE,
    )
    residual = x_full + attn_share + vector_rows[4]
    normed2, inv2 = norm_rows(residual)
    h_two = lax.all_gather(
        (normed2 * vector_rows[5] + vector_rows[6]).astype(HALF_TYPE), "tensor", axis=0, tiled=True
    )
    pre_act = jnp.dot(h_two, w_up, preferred_element_type=FULL_TYPE) + up_bias
    activation = gelu_value(pre_act).astype(HALF_TYPE)
    part_rows = activation
    mlp_share = tensor_scatter(
        lax.dot_general(
            part_rows, w_down, (((1,), (1,)), ((), ())), preferred_element_type=FULL_TYPE
        ),
        HALF_TYPE,
    )
    output = jnp.where(valid[:, None], residual + mlp_share + vector_rows[down_row], 0.0)
    grad_out = jnp.where(valid[:, None], cotangent.astype(FULL_TYPE), 0.0)
    grad_rows = lax.all_gather(grad_out.astype(HALF_TYPE), "tensor", axis=0, tiled=True)
    grad_pre = jnp.dot(grad_rows, w_down, preferred_element_type=FULL_TYPE) * gelu_slope(pre_act)
    grad_pre_half = grad_pre.astype(HALF_TYPE)
    grad_down = lax.dot_general(
        grad_rows, activation, (((0,), (0,)), ((), ())), preferred_element_type=FULL_TYPE
    ).astype(HALF_TYPE)
    grad_up = lax.dot_general(
        h_two, grad_pre_half, (((0,), (0,)), ((), ())), preferred_element_type=FULL_TYPE
    ).astype(HALF_TYPE)
    grad_up_bias = jnp.sum(grad_pre, axis=0)
    part_rows = grad_pre_half
    grad_h2 = tensor_scatter(
        lax.dot_general(
            part_rows, w_up, (((1,), (1,)), ((), ())), preferred_element_type=FULL_TYPE
        ),
        FULL_TYPE,
    )
    grad_resid = grad_out + norm_back(grad_h2, normed2, inv2, vector_rows[5])
    grad_mixed_rows = lax.all_gather(grad_resid.astype(HALF_TYPE), "tensor", axis=0, tiled=True)
    grad_outw = lax.dot_general(
        grad_mixed_rows, mixed_heads, (((0,), (0,)), ((), ())), preferred_element_type=FULL_TYPE
    ).astype(HALF_TYPE)
    grad_mixed = (
        jnp.dot(grad_mixed_rows, w_out, preferred_element_type=FULL_TYPE)
        .astype(HALF_TYPE)
        .reshape(group_rows, local_heads, HEAD_DIM)
    )
    mixed_split = mixed_heads.reshape(group_rows, local_heads, HEAD_DIM)
    delta_rows = jnp.einsum(
        "qhd,qhd->hq", grad_mixed, mixed_split, preferred_element_type=FULL_TYPE
    )
    scores = score_table(queries, key_rows, slopes, labels)
    prob_table = jnp.exp(scores - log_total)
    prob_half = prob_table.astype(HALF_TYPE)
    grad_probs = jnp.einsum("qhd,khd->hqk", grad_mixed, values, preferred_element_type=FULL_TYPE)
    grad_scores = (prob_table * (grad_probs - delta_rows[:, :, None])).astype(HALF_TYPE)
    grad_q = (
        jnp.einsum("hqk,khd->qhd", grad_scores, key_rows, preferred_element_type=FULL_TYPE)
        * inv_scale
    )
    grad_k = (
        jnp.einsum("hqk,qhd->khd", grad_scores, queries, preferred_element_type=FULL_TYPE)
        * inv_scale
    )
    grad_v = jnp.einsum("hqk,qhd->khd", prob_half, grad_mixed, preferred_element_type=FULL_TYPE)
    grad_proj = jnp.stack([grad_q, grad_k, grad_v]).reshape(3, group_rows, head_cols)
    grad_proj_half = grad_proj.astype(HALF_TYPE)
    grad_qkv = [
        lax.dot_general(
            h_one, grad_proj_half[c], (((0,), (0,)), ((), ())), preferred_element_type=FULL_TYPE
        ).astype(HALF_TYPE)
        for c in range(3)
    ]
    part_rows = grad_proj_half
    grad_h1 = tensor_scatter(
        sum(
            lax.dot_general(
                part_rows[c], w_qkv[c], (((1,), (1,)), ((), ())), preferred_element_type=FULL_TYPE
            )
            for c in range(3)
        ),
        FULL_TYPE,
    )
    input_grad = grad_resid + norm_back(grad_h1, normed1, inv1, vector_rows[0])
    empty_row = jnp.zeros((model_width,), FULL_TYPE)
    q_row = lax.dynamic_update_slice_in_dim(
        empty_row, jnp.sum(grad_proj[0], axis=0), tensor_index * head_cols, 0
    )
    v_row = lax.dynamic_update_slice_in_dim(
        empty_row, jnp.sum(grad_proj[2], axis=0), tensor_index * head_cols, 0
    )
    up_part = lax.dynamic_update_slice_in_dim(
        jnp.zeros((up_rows * model_width,), FULL_TYPE), grad_up_bias, tensor_index * hidden_cols, 0
    ).reshape(up_rows, model_width)
    head_part = jnp.stack(
        [
            jnp.sum(grad_h1 * normed1, axis=0),
            jnp.sum(grad_h1, axis=0),
            q_row,
            v_row,
            jnp.sum(grad_resid, axis=0),
            jnp.sum(grad_h2 * normed2, axis=0),
            jnp.sum(grad_h2, axis=0),
        ]
    )
    grad_vec = jnp.concatenate([head_part, up_part, jnp.sum(grad_out, axis=0)[None]], axis=0)
    lead = tuple(factors)
    vec_table = jnp.pad(
        grad_vec.reshape(vec_rows, dp_size, vec_cols).transpose(1, 0, 2).astype(HALF_TYPE),
        ((0, 0), (0, pad_rows), (0, head_cols - vec_cols)),
    )
    tables = [piece.reshape(dp_size, shard, head_cols) for piece in grad_qkv + [grad_outw]]
    near_sums = [
        jnp.concatenate([tables[0], tables[1], vec_table], axis=1),
        jnp.concatenate([tables[2], tables[3]], axis=1),
    ]
    near_sums = [piece.reshape(lead + piece.shape[1:]) for piece in near_sums]
    far_sums = [piece.reshape(lead + (shard, hidden_cols)) for piece in (grad_up, grad_down)]
    for step in reversed(range(1, stages)):
        far_sums = [
            scatter_stage(piece, orders[i][step], dp_size) for i, piece in enumerate(far_sums)
        ]
    far_sum = scatter_stage(jnp.concatenate(far_sums, axis=-2), 0, dp_size)
    for step in reversed(range(1, stages)):
        near_sums = [
            scatter_stage(piece, orders[i][step], dp_size) for i, piece in enumerate(near_sums)
        ]
    near_sum = scatter_stage(jnp.concatenate(near_sums, axis=-2), 0, dp_size)
    near_sum = near_sum.reshape(-1, head_cols)
    first_sum, second_sum = near_sum[:near_rows], near_sum[near_rows:]
    far_sum = far_sum.reshape(-1, hidden_cols)
    sum_qkv = jnp.stack([first_sum[:shard], first_sum[shard : 2 * shard], second_sum[:shard]])
    sum_out = second_sum[shard:]
    sum_up = far_sum[:shard]
    sum_down = far_sum[shard:]
    sum_vec = first_sum[2 * shard : 2 * shard + vec_rows, :vec_cols]
    sum_vec = lax.psum(sum_vec, "tensor")
    qkv_grad = sum_qkv / token_total
    out_grad = sum_out / token_total
    fc1_grad = sum_up / token_total
    fc2_grad = sum_down / token_total
    vector_grad = sum_vec / token_total
    qkv_new, qkv_first_new, qkv_second_new = adam_step(
        qkv_weight, qkv_first, qkv_second, qkv_grad, DECAY_RATE
    )
    out_new, out_first_new, out_second_new = adam_step(
        out_weight, out_first, out_second, out_grad, DECAY_RATE
    )
    fc1_new, fc1_first_new, fc1_second_new = adam_step(
        fc1_weight, fc1_first, fc1_second, fc1_grad, DECAY_RATE
    )
    fc2_new, fc2_first_new, fc2_second_new = adam_step(
        fc2_weight, fc2_first, fc2_second, fc2_grad, DECAY_RATE
    )
    vector_new, vector_first_new, vector_second_new = adam_step(
        vectors, vector_first, vector_second, vector_grad, 0.0
    )
    return (
        output,
        input_grad,
        qkv_grad,
        out_grad,
        fc1_grad,
        fc2_grad,
        vector_grad,
        qkv_new,
        out_new,
        fc1_new,
        fc2_new,
        vector_new,
        qkv_first_new,
        qkv_second_new,
        out_first_new,
        out_second_new,
        fc1_first_new,
        fc1_second_new,
        fc2_first_new,
        fc2_second_new,
        vector_first_new,
        vector_second_new,
    )


def solution(mesh):
    in_specs = (
        P(("dp", "tensor"), None),
        P(("dp", "tensor"), None),
        P("dp", None),
        P("dp", None),
        P(),
        P(None, "dp", "tensor"),
        P("dp", "tensor"),
        P("dp", "tensor"),
        P("dp", "tensor"),
        P(None, "dp"),
        P(None, "dp", "tensor"),
        P(None, "dp", "tensor"),
        P("dp", "tensor"),
        P("dp", "tensor"),
        P("dp", "tensor"),
        P("dp", "tensor"),
        P("dp", "tensor"),
        P("dp", "tensor"),
        P(None, "dp"),
        P(None, "dp"),
    )
    out_specs = (
        P(("dp", "tensor"), None),
        P(("dp", "tensor"), None),
        P(None, "dp", "tensor"),
        P("dp", "tensor"),
        P("dp", "tensor"),
        P("dp", "tensor"),
        P(None, "dp"),
        P(None, "dp", "tensor"),
        P("dp", "tensor"),
        P("dp", "tensor"),
        P("dp", "tensor"),
        P(None, "dp"),
        P(None, "dp", "tensor"),
        P(None, "dp", "tensor"),
        P("dp", "tensor"),
        P("dp", "tensor"),
        P("dp", "tensor"),
        P("dp", "tensor"),
        P("dp", "tensor"),
        P("dp", "tensor"),
        P(None, "dp"),
        P(None, "dp"),
    )
    return jax.shard_map(local, mesh=mesh, in_specs=in_specs, out_specs=out_specs, check_vma=False)
```

```python
import jax
import jax.numpy as jnp
from jax import lax
from jax.sharding import PartitionSpec as P


HEADS = 16
HEAD_DIM = 64
STEP = 3


HALF_TYPE = jnp.bfloat16
FULL_TYPE = jnp.float32
GELU_SCALE = 0.7978845608028654
GELU_CUBIC = 0.044715
NORM_EPS = 1e-05
BETA_ONE = 0.9
BETA_TWO = 0.95
LEARN_RATE = 0.05
DECAY_RATE = 0.1
ADAM_EPS = 1e-08
NEG_LARGE = -1e30


def axis_plan(size):
    factors, rest = [], size
    if rest % 4 == 0:
        factors.append(4)
        rest //= 4
    divisor = 2
    while rest > 1:
        while rest % divisor == 0:
            factors.append(divisor)
            rest //= divisor
        divisor += 1
    strides, stride = [], size
    for factor in factors:
        stride //= factor
        strides.append(stride)
    return factors, strides


def moves(size, factor, stride, step):
    pairs = []
    for source in range(size):
        coord = (source // stride) % factor
        pairs.append((source, source + ((coord + step) % factor - coord) * stride))
    return pairs


def after(values, earlier):
    return lax.optimization_barrier((values, earlier))[0]


def gather_send(block, place, size):
    factors, strides = axis_plan(size)
    factor, stride = factors[place], strides[place]
    return [block] + [
        lax.ppermute(block, "dp", moves(size, factor, stride, step)) for step in range(1, factor)
    ]


def gather_place(held, place, size):
    factors, strides = axis_plan(size)
    factor, stride = factors[place], strides[place]
    coord = (lax.axis_index("dp") // stride) % factor
    parts = []
    for slot in range(factor):
        part = held[0]
        for step in range(1, factor):
            part = jnp.where(coord == (slot + step) % factor, held[step], part)
        parts.append(part)
    return jnp.concatenate(parts, axis=place)


def scatter_axis(table, place, factor, stride, size):
    coord = (lax.axis_index("dp") // stride) % factor

    def take(step):
        return lax.dynamic_slice_in_dim(table, (coord + step) % factor, 1, axis=place)

    total = take(0).astype(FULL_TYPE)
    for step in range(1, factor):
        away = take(step).astype(HALF_TYPE)
        other = lax.ppermute(away, "dp", moves(size, factor, stride, step))
        total = total + other.astype(FULL_TYPE)
    return total


def stage_orders(count):
    forward = list(range(count))
    return [forward, forward[:1] + forward[1:][::-1]]


def gather_stage(block, place, size):
    return gather_place(gather_send(block, place, size), place, size)


def scatter_stage(table, place, size):
    factors, strides = axis_plan(size)
    return scatter_axis(table, place, factors[place], strides[place], size)


def tensor_scatter(rows, send_type):
    size = lax.axis_size("tensor")
    if size != 2:
        return lax.psum_scatter(rows, "tensor", scatter_dimension=0, tiled=True)
    half = rows.shape[0] // 2
    index = lax.axis_index("tensor")
    own = lax.dynamic_slice_in_dim(rows, index * half, half)
    away = lax.dynamic_slice_in_dim(rows, (1 - index) * half, half).astype(send_type)
    return own + lax.ppermute(away, "tensor", [(0, 1), (1, 0)]).astype(FULL_TYPE)


def norm_rows(matrix):
    center = matrix - jnp.mean(matrix, axis=-1, keepdims=True)
    inv_root = lax.rsqrt(jnp.mean(center * center, axis=-1, keepdims=True) + NORM_EPS)
    return (center * inv_root, inv_root)


def norm_back(gradient, normed, inv_root, gain):
    inner_grad = gradient * gain
    return inv_root * (
        inner_grad
        - jnp.mean(inner_grad, axis=-1, keepdims=True)
        - normed * jnp.mean(inner_grad * normed, axis=-1, keepdims=True)
    )


def gelu_value(pre_act):
    return (
        0.5
        * pre_act
        * (1.0 + jnp.tanh(GELU_SCALE * (pre_act + GELU_CUBIC * pre_act * pre_act * pre_act)))
    )


def gelu_slope(pre_act):
    tangent = jnp.tanh(GELU_SCALE * (pre_act + GELU_CUBIC * pre_act * pre_act * pre_act))
    return 0.5 * (1.0 + tangent) + 0.5 * pre_act * (1.0 - tangent * tangent) * GELU_SCALE * (
        1.0 + 3.0 * GELU_CUBIC * pre_act * pre_act
    )


def row_labels(lengths, offsets, group_rows):
    places = jnp.arange(group_rows, dtype=jnp.int32)[:, None]
    inside = (places >= offsets[None, :]) & (places < offsets[None, :] + lengths[None, :])
    rank_ids = jnp.arange(lengths.shape[0], dtype=jnp.int32)[None, :] + 1
    return jnp.sum(jnp.where(inside, rank_ids, 0), axis=1) - 1


def score_table(queries, key_rows, slopes, labels):
    raw_scores = jnp.einsum(
        "qhd,khd->hqk", queries, key_rows, preferred_element_type=FULL_TYPE
    ) * queries.shape[2] ** (-0.5)
    places = jnp.arange(queries.shape[0], dtype=jnp.int32)
    row_gap = places[:, None] - places[None, :]
    allowed = (labels[:, None] == labels[None, :]) & (row_gap >= 0)
    return jnp.where(
        allowed[None],
        raw_scores - slopes[:, None, None] * row_gap.astype(FULL_TYPE)[None],
        NEG_LARGE,
    )


def adam_step(weight, first_moment, second_moment, gradient, decay_rate):
    first_new = BETA_ONE * first_moment + (1.0 - BETA_ONE) * gradient
    second_new = BETA_TWO * second_moment + (1.0 - BETA_TWO) * gradient * gradient
    first_hat = first_new / (1.0 - BETA_ONE**STEP)
    second_hat = second_new / (1.0 - BETA_TWO**STEP)
    weight_new = weight - LEARN_RATE * (
        first_hat / (jnp.sqrt(second_hat) + ADAM_EPS) + decay_rate * weight
    )
    return (weight_new, first_new, second_new)


def local(
    tokens,
    cotangent,
    seq_lengths,
    seq_offsets,
    token_counts,
    qkv_weight,
    out_weight,
    fc1_weight,
    fc2_weight,
    vectors,
    qkv_first,
    qkv_second,
    out_first,
    out_second,
    fc1_first,
    fc1_second,
    fc2_first,
    fc2_second,
    vector_first,
    vector_second,
):
    tensor_size = lax.axis_size("tensor")
    tensor_index = lax.axis_index("tensor")
    share_rows = tokens.shape[0]
    group_rows = share_rows * tensor_size
    model_width = tokens.shape[1]
    head_cols = qkv_weight.shape[2]
    hidden_cols = fc1_weight.shape[1]
    local_heads = head_cols // HEAD_DIM
    up_rows = hidden_cols * tensor_size // model_width
    down_row = 7 + up_rows
    inv_scale = HEAD_DIM ** (-0.5)
    dp_size = lax.axis_size("dp")
    factors, _ = axis_plan(dp_size)
    stages = len(factors)
    ones = (1,) * stages
    orders = stage_orders(stages)
    shard = qkv_weight.shape[1]
    vec_rows, vec_cols = vectors.shape
    pad_rows = -vec_rows % 16
    vec_block = jnp.pad(
        vectors.astype(HALF_TYPE), ((0, pad_rows), (0, head_cols - vec_cols))
    )
    qkv_half = qkv_weight.astype(HALF_TYPE)
    near = [
        jnp.concatenate([qkv_half[0], qkv_half[1], vec_block], axis=0),
        jnp.concatenate([qkv_half[2], out_weight.astype(HALF_TYPE)], axis=0),
    ]
    far = [fc1_weight.astype(HALF_TYPE), fc2_weight.astype(HALF_TYPE)]
    near = [block.reshape(ones + block.shape) for block in near]
    far = [block.reshape(ones + block.shape) for block in far]
    near_rows = near[0].shape[-2]
    near = gather_send(jnp.concatenate(near, axis=-2), 0, dp_size)
    far = after(far, near[1])
    near = gather_place(near, 0, dp_size)
    near = [near[..., :near_rows, :], near[..., near_rows:, :]]
    far = gather_send(jnp.concatenate(far, axis=-2), 0, dp_size)
    for step in range(1, stages):
        near = [gather_send(block, orders[i][step], dp_size) for i, block in enumerate(near)]
        if step == stages - 1:
            far = after(far, near)
        near = [gather_place(held, orders[i][step], dp_size) for i, held in enumerate(near)]
    far = gather_place(far, 0, dp_size)
    far = [far[..., :shard, :], far[..., shard:, :]]
    for step in range(1, stages - 1):
        far = [gather_stage(block, orders[i][step], dp_size) for i, block in enumerate(far)]
    full_rows = dp_size * shard
    first = near[0].reshape(dp_size, -1, head_cols)
    second = near[1].reshape(dp_size, -1, head_cols)
    w_qkv = [
        first[:, :shard].reshape(full_rows, head_cols),
        first[:, shard : 2 * shard].reshape(full_rows, head_cols),
        second[:, :shard].reshape(full_rows, head_cols),
    ]
    w_out = second[:, shard:].reshape(full_rows, head_cols)
    vector_half = (
        first[:, 2 * shard : 2 * shard + vec_rows, :vec_cols]
        .transpose(1, 0, 2)
        .reshape(vec_rows, dp_size * vec_cols)
    )
    vector_rows = vector_half.astype(FULL_TYPE)
    q_bias = lax.dynamic_slice_in_dim(vector_rows[2], tensor_index * head_cols, head_cols)
    v_bias = lax.dynamic_slice_in_dim(vector_rows[3], tensor_index * head_cols, head_cols)
    up_bias = lax.dynamic_slice_in_dim(
        vector_rows[7:down_row].reshape(-1), tensor_index * hidden_cols, hidden_cols
    )
    labels = row_labels(seq_lengths[0], seq_offsets[0], group_rows)
    share_start = tensor_index * share_rows
    share_labels = lax.dynamic_slice_in_dim(labels, share_start, share_rows)
    count_now = lax.dynamic_index_in_dim(token_counts, lax.axis_index("dp"), 0, keepdims=False)
    share_places = share_start + jnp.arange(share_rows, dtype=jnp.int32)
    valid = (share_labels >= 0) & (share_places < count_now)
    token_total = jnp.sum(token_counts).astype(FULL_TYPE)
    slopes = jnp.exp2(
        -8.0 * (tensor_index * local_heads + jnp.arange(local_heads) + 1).astype(FULL_TYPE) / HEADS
    )
    x_full = tokens.astype(FULL_TYPE)
    normed1, inv1 = norm_rows(x_full)
    h_one = lax.all_gather(
        (normed1 * vector_rows[0] + vector_rows[1]).astype(HALF_TYPE), "tensor", axis=0, tiled=True
    )
    projected = [jnp.dot(h_one, w, preferred_element_type=FULL_TYPE) for w in w_qkv]
    queries = (projected[0] + q_bias).astype(HALF_TYPE).reshape(group_rows, local_heads, HEAD_DIM)
    key_rows = projected[1].astype(HALF_TYPE).reshape(group_rows, local_heads, HEAD_DIM)
    values = (projected[2] + v_bias).astype(HALF_TYPE).reshape(group_rows, local_heads, HEAD_DIM)
    scores = score_table(queries, key_rows, slopes, labels)
    row_peak = jnp.max(scores, axis=2, keepdims=True)
    log_total = row_peak + jnp.log(jnp.sum(jnp.exp(scores - row_peak), axis=2, keepdims=True))
    prob_half = jnp.exp(scores - log_total).astype(HALF_TYPE)
    mixed_heads = (
        jnp.einsum("hqk,khd->qhd", prob_half, values, preferred_element_type=FULL_TYPE)
        .astype(HALF_TYPE)
        .reshape(group_rows, head_cols)
    )
    part_rows = mixed_heads
    attn_share = tensor_scatter(
        lax.dot_general(
            part_rows, w_out, (((1,), (1,)), ((), ())), preferred_element_type=FULL_TYPE
        ),
        FULL_TYPE,
    )
    attn_share, far = lax.optimization_barrier((attn_share, far))
    if stages > 1:
        far = [gather_stage(block, orders[i][-1], dp_size) for i, block in enumerate(far)]
    w_up = far[0].reshape(full_rows, hidden_cols)
    w_down = far[1].reshape(full_rows, hidden_cols)
    residual = x_full + attn_share + vector_rows[4]
    normed2, inv2 = norm_rows(residual)
    h_two = lax.all_gather(
        (normed2 * vector_rows[5] + vector_rows[6]).astype(HALF_TYPE), "tensor", axis=0, tiled=True
    )
    pre_act = jnp.dot(h_two, w_up, preferred_element_type=FULL_TYPE) + up_bias
    activation = gelu_value(pre_act).astype(HALF_TYPE)
    part_rows = activation
    mlp_share = tensor_scatter(
        lax.dot_general(
            part_rows, w_down, (((1,), (1,)), ((), ())), preferred_element_type=FULL_TYPE
        ),
        HALF_TYPE,
    )
    output = jnp.where(valid[:, None], residual + mlp_share + vector_rows[down_row], 0.0)
    grad_out = jnp.where(valid[:, None], cotangent.astype(FULL_TYPE), 0.0)
    grad_rows = lax.all_gather(grad_out.astype(HALF_TYPE), "tensor", axis=0, tiled=True)
    grad_pre = jnp.dot(grad_rows, w_down, preferred_element_type=FULL_TYPE) * gelu_slope(pre_act)
    grad_pre_half = grad_pre.astype(HALF_TYPE)
    grad_down = lax.dot_general(
        grad_rows, activation, (((0,), (0,)), ((), ())), preferred_element_type=FULL_TYPE
    ).astype(HALF_TYPE)
    grad_up = lax.dot_general(
        h_two, grad_pre_half, (((0,), (0,)), ((), ())), preferred_element_type=FULL_TYPE
    ).astype(HALF_TYPE)
    grad_up_bias = jnp.sum(grad_pre, axis=0)
    part_rows = grad_pre_half
    grad_h2 = tensor_scatter(
        lax.dot_general(
            part_rows, w_up, (((1,), (1,)), ((), ())), preferred_element_type=FULL_TYPE
        ),
        FULL_TYPE,
    )
    grad_resid = grad_out + norm_back(grad_h2, normed2, inv2, vector_rows[5])
    grad_mixed_rows = lax.all_gather(grad_resid.astype(HALF_TYPE), "tensor", axis=0, tiled=True)
    grad_outw = lax.dot_general(
        grad_mixed_rows, mixed_heads, (((0,), (0,)), ((), ())), preferred_element_type=FULL_TYPE
    ).astype(HALF_TYPE)
    grad_mixed = (
        jnp.dot(grad_mixed_rows, w_out, preferred_element_type=FULL_TYPE)
        .astype(HALF_TYPE)
        .reshape(group_rows, local_heads, HEAD_DIM)
    )
    mixed_split = mixed_heads.reshape(group_rows, local_heads, HEAD_DIM)
    delta_rows = jnp.einsum(
        "qhd,qhd->hq", grad_mixed, mixed_split, preferred_element_type=FULL_TYPE
    )
    scores = score_table(queries, key_rows, slopes, labels)
    prob_table = jnp.exp(scores - log_total)
    prob_half = prob_table.astype(HALF_TYPE)
    grad_probs = jnp.einsum("qhd,khd->hqk", grad_mixed, values, preferred_element_type=FULL_TYPE)
    grad_scores = (prob_table * (grad_probs - delta_rows[:, :, None])).astype(HALF_TYPE)
    grad_q = (
        jnp.einsum("hqk,khd->qhd", grad_scores, key_rows, preferred_element_type=FULL_TYPE)
        * inv_scale
    )
    grad_k = (
        jnp.einsum("hqk,qhd->khd", grad_scores, queries, preferred_element_type=FULL_TYPE)
        * inv_scale
    )
    grad_v = jnp.einsum("hqk,qhd->khd", prob_half, grad_mixed, preferred_element_type=FULL_TYPE)
    grad_proj = jnp.stack([grad_q, grad_k, grad_v]).reshape(3, group_rows, head_cols)
    grad_proj_half = grad_proj.astype(HALF_TYPE)
    grad_qkv = [
        lax.dot_general(
            h_one, grad_proj_half[c], (((0,), (0,)), ((), ())), preferred_element_type=FULL_TYPE
        ).astype(HALF_TYPE)
        for c in range(3)
    ]
    part_rows = grad_proj_half
    grad_h1 = tensor_scatter(
        sum(
            lax.dot_general(
                part_rows[c], w_qkv[c], (((1,), (1,)), ((), ())), preferred_element_type=FULL_TYPE
            )
            for c in range(3)
        ),
        FULL_TYPE,
    )
    input_grad = grad_resid + norm_back(grad_h1, normed1, inv1, vector_rows[0])
    empty_row = jnp.zeros((model_width,), FULL_TYPE)
    q_row = lax.dynamic_update_slice_in_dim(
        empty_row, jnp.sum(grad_proj[0], axis=0), tensor_index * head_cols, 0
    )
    v_row = lax.dynamic_update_slice_in_dim(
        empty_row, jnp.sum(grad_proj[2], axis=0), tensor_index * head_cols, 0
    )
    up_part = lax.dynamic_update_slice_in_dim(
        jnp.zeros((up_rows * model_width,), FULL_TYPE), grad_up_bias, tensor_index * hidden_cols, 0
    ).reshape(up_rows, model_width)
    head_part = jnp.stack(
        [
            jnp.sum(grad_h1 * normed1, axis=0),
            jnp.sum(grad_h1, axis=0),
            q_row,
            v_row,
            jnp.sum(grad_resid, axis=0),
            jnp.sum(grad_h2 * normed2, axis=0),
            jnp.sum(grad_h2, axis=0),
        ]
    )
    grad_vec = jnp.concatenate([head_part, up_part, jnp.sum(grad_out, axis=0)[None]], axis=0)
    lead = tuple(factors)
    vec_table = jnp.pad(
        grad_vec.reshape(vec_rows, dp_size, vec_cols).transpose(1, 0, 2).astype(HALF_TYPE),
        ((0, 0), (0, pad_rows), (0, head_cols - vec_cols)),
    )
    tables = [piece.reshape(dp_size, shard, head_cols) for piece in grad_qkv + [grad_outw]]
    near_sums = [
        jnp.concatenate([tables[0], tables[1], vec_table], axis=1),
        jnp.concatenate([tables[2], tables[3]], axis=1),
    ]
    near_sums = [piece.reshape(lead + piece.shape[1:]) for piece in near_sums]
    far_sums = [piece.reshape(lead + (shard, hidden_cols)) for piece in (grad_up, grad_down)]
    for step in reversed(range(1, stages)):
        far_sums = [
            scatter_stage(piece, orders[i][step], dp_size) for i, piece in enumerate(far_sums)
        ]
        if step == 1:
            near_sums = after(near_sums, far_sums)
    far_sum = scatter_stage(jnp.concatenate(far_sums, axis=-2), 0, dp_size)
    for step in reversed(range(1, stages)):
        near_sums = [
            scatter_stage(piece, orders[i][step], dp_size) for i, piece in enumerate(near_sums)
        ]
    near_sum = scatter_stage(jnp.concatenate(near_sums, axis=-2), 0, dp_size)
    near_sum = near_sum.reshape(-1, head_cols)
    first_sum, second_sum = near_sum[:near_rows], near_sum[near_rows:]
    far_sum = far_sum.reshape(-1, hidden_cols)
    sum_qkv = jnp.stack([first_sum[:shard], first_sum[shard : 2 * shard], second_sum[:shard]])
    sum_out = second_sum[shard:]
    sum_up = far_sum[:shard]
    sum_down = far_sum[shard:]
    sum_vec = first_sum[2 * shard : 2 * shard + vec_rows, :vec_cols]
    sum_vec = lax.psum(sum_vec, "tensor")
    qkv_grad = sum_qkv / token_total
    out_grad = sum_out / token_total
    fc1_grad = sum_up / token_total
    fc2_grad = sum_down / token_total
    vector_grad = sum_vec / token_total
    qkv_new, qkv_first_new, qkv_second_new = adam_step(
        qkv_weight, qkv_first, qkv_second, qkv_grad, DECAY_RATE
    )
    out_new, out_first_new, out_second_new = adam_step(
        out_weight, out_first, out_second, out_grad, DECAY_RATE
    )
    fc1_new, fc1_first_new, fc1_second_new = adam_step(
        fc1_weight, fc1_first, fc1_second, fc1_grad, DECAY_RATE
    )
    fc2_new, fc2_first_new, fc2_second_new = adam_step(
        fc2_weight, fc2_first, fc2_second, fc2_grad, DECAY_RATE
    )
    vector_new, vector_first_new, vector_second_new = adam_step(
        vectors, vector_first, vector_second, vector_grad, 0.0
    )
    return (
        output,
        input_grad,
        qkv_grad,
        out_grad,
        fc1_grad,
        fc2_grad,
        vector_grad,
        qkv_new,
        out_new,
        fc1_new,
        fc2_new,
        vector_new,
        qkv_first_new,
        qkv_second_new,
        out_first_new,
        out_second_new,
        fc1_first_new,
        fc1_second_new,
        fc2_first_new,
        fc2_second_new,
        vector_first_new,
        vector_second_new,
    )


def solution(mesh):
    in_specs = (
        P(("dp", "tensor"), None),
        P(("dp", "tensor"), None),
        P("dp", None),
        P("dp", None),
        P(),
        P(None, "dp", "tensor"),
        P("dp", "tensor"),
        P("dp", "tensor"),
        P("dp", "tensor"),
        P(None, "dp"),
        P(None, "dp", "tensor"),
        P(None, "dp", "tensor"),
        P("dp", "tensor"),
        P("dp", "tensor"),
        P("dp", "tensor"),
        P("dp", "tensor"),
        P("dp", "tensor"),
        P("dp", "tensor"),
        P(None, "dp"),
        P(None, "dp"),
    )
    out_specs = (
        P(("dp", "tensor"), None),
        P(("dp", "tensor"), None),
        P(None, "dp", "tensor"),
        P("dp", "tensor"),
        P("dp", "tensor"),
        P("dp", "tensor"),
        P(None, "dp"),
        P(None, "dp", "tensor"),
        P("dp", "tensor"),
        P("dp", "tensor"),
        P("dp", "tensor"),
        P(None, "dp"),
        P(None, "dp", "tensor"),
        P(None, "dp", "tensor"),
        P("dp", "tensor"),
        P("dp", "tensor"),
        P("dp", "tensor"),
        P("dp", "tensor"),
        P("dp", "tensor"),
        P("dp", "tensor"),
        P(None, "dp"),
        P(None, "dp"),
    )
    return jax.shard_map(local, mesh=mesh, in_specs=in_specs, out_specs=out_specs, check_vma=False)
```
